32 devices in a mesh: aux: 8 (over z, core), grp: 4 (over y, x).
Axes of the slice: x: 2, y: 2, z: 4, core: 2. Of those that a mesh axis runs over, the one named last changes fastest.
Arguments:
- integrals: bfloat16 [1024, 512, 256], P('aux', 'grp'), may hold values from -2.5 to 2.5
- metric: bfloat16 [1024, 1024], replicated, may hold values from -0.1875 to 0.1875
- fock: bfloat16 [512, 512], replicated, may hold values from -2 to 0.5, as said below
- virt_energy: float32 [256], replicated, may hold values from 0.3 to 3
- send_orb: int32 [32, 4], P(('aux', 'grp')), may hold values from 0 to 15, as said below
- pair_orb: int32 [512, 2], P(('aux', 'grp')), may hold values from 0 to 511, as said below
- send_pair: int32 [32, 4], P(('aux', 'grp')), may hold values from 0 to 15, as said below
- cpl_slot: int32 [512, 4], P(('aux', 'grp')), may hold values from 0 to 3, as said below
- cpl_orb: int32 [512, 4, 2], P(('aux', 'grp')), may hold values from 0 to 511, as said below
Outputs:
- amplitudes: float32 [512, 256, 256], P(('aux', 'grp'))
The draws below stay inside these ranges and needn't reach their ends.
Inputs may be any that keep to these rules, and one draw needn't show every extreme that they name: send_orb is below 16. `pair_orb`: the orbitals of the pairs owned by device (col, g) lie in column col: an orbital o of them has (o % 128) // 16 == col and o % 16 == send_orb[col * 4 + o // 128, g]. No pair is listed twice on a device. send_pair indexes the sending device's own pairs. `cpl_slot`: the entries of one pair are distinct. cpl_orb[p, e] equals pair_orb of the pair q[p, e] defined in the reference program. fock is symmetric with diagonal entries between -2 and -0.5.
All inputs are finite; a program needn't handle non-finite values.
Results may differ from the reference program's by a relative error of at most 0.0027.
Values may be sent and summed in bfloat16 or wider, within the bound.
A program may use at most 128 MiB of HBM per device.

```python
import math
import jax
import jax.numpy as jnp
from jax import lax

NAUX = 1024
NOCC = 512
NV = 256
PAIRS = 16
NC = 4
ITERS = 2
N_AUX = 8
N_GRP = 4


def routing(key):
    base = jax.random.fold_in(key, 9173)
    keys = jax.random.split(base, 4)
    ndev = N_AUX * N_GRP
    orb_dev = NOCC // ndev
    group_orbs = NOCC // N_GRP
    grid = N_GRP * N_GRP
    send_orb = jax.random.randint(keys[0], (N_AUX, N_GRP, N_GRP), 0, orb_dev).astype(jnp.int32)
    col_base = jnp.arange(N_AUX, dtype=jnp.int32)[:, None, None] * orb_dev
    grp_base = jnp.arange(N_GRP, dtype=jnp.int32)[None, :, None] * group_orbs
    slot_orb = grp_base + col_base + send_orb
    received = jnp.transpose(slot_orb, (0, 2, 1))
    noise = jax.random.randint(keys[1], (N_AUX, N_GRP, grid), 0, 1 << 20)
    order = jnp.argsort(noise * grid + jnp.arange(grid, dtype=jnp.int32), axis=-1)[:, :, :PAIRS]
    orb_first = jnp.take_along_axis(received, order // N_GRP, axis=2)
    orb_second = jnp.take_along_axis(received, order % N_GRP, axis=2)
    left_i = orb_first[:, :, :, None, None]
    left_j = orb_second[:, :, :, None, None]
    right_k = orb_first[:, None, None, :, :]
    right_l = orb_second[:, None, None, :, :]
    share = (right_l == left_j) & (right_k != left_i) | (right_k == left_i) & (right_l != left_j)
    count = jnp.sum(share.astype(jnp.int32), axis=2)
    tie = jax.random.randint(keys[2], (N_AUX, N_GRP, N_GRP, PAIRS), 0, 1 << 10)
    score = count * (1 << 20) + tie * PAIRS + jnp.arange(PAIRS, dtype=jnp.int32)
    best = jnp.argmax(score, axis=-1).astype(jnp.int32)
    send_pair = jnp.transpose(best, (0, 2, 1))
    pick = best[..., None] == jnp.arange(PAIRS, dtype=jnp.int32)
    sent_first = jnp.sum(jnp.where(pick, orb_first[:, None, :, :], 0), axis=-1)
    sent_second = jnp.sum(jnp.where(pick, orb_second[:, None, :, :], 0), axis=-1)
    own_i = orb_first[..., None]
    own_j = orb_second[..., None]
    got_k = sent_first[:, :, None, :]
    got_l = sent_second[:, :, None, :]
    share_two = (got_l == own_j) & (got_k != own_i) | (got_k == own_i) & (got_l != own_j)
    tie_two = jax.random.randint(keys[3], (N_AUX, N_GRP, PAIRS, N_GRP), 0, 1 << 10)
    score_two = share_two.astype(jnp.int32) * (1 << 20) + tie_two * N_GRP + jnp.arange(N_GRP, dtype=jnp.int32)
    unused, chosen = lax.top_k(score_two, NC)
    chosen = chosen.astype(jnp.int32)
    shape_full = (N_AUX, N_GRP, PAIRS, N_GRP)
    cpl_first = jnp.take_along_axis(jnp.broadcast_to(got_k, shape_full), chosen, axis=3)
    cpl_second = jnp.take_along_axis(jnp.broadcast_to(got_l, shape_full), chosen, axis=3)
    pair_orb = jnp.stack([orb_first, orb_second], axis=-1).reshape(ndev * PAIRS, 2)
    cpl_orb = jnp.stack([cpl_first, cpl_second], axis=-1).reshape(ndev * PAIRS, NC, 2)
    return (send_orb.reshape(ndev, N_GRP).astype(jnp.int32), pair_orb.astype(jnp.int32), send_pair.reshape(ndev, N_GRP).astype(jnp.int32), chosen.reshape(ndev * PAIRS, NC), cpl_orb.astype(jnp.int32))


def draw_send_orb(key, part):
    return routing(key)[0]


def draw_pair_orb(key, part):
    return routing(key)[1]


def draw_send_pair(key, part):
    return routing(key)[2]


def draw_cpl_slot(key, part):
    return routing(key)[3]


def draw_cpl_orb(key, part):
    return routing(key)[4]


def draw_fock(key, part):
    base = jax.random.fold_in(key, 311)
    key_off, key_diag = jax.random.split(base)
    raw = jnp.clip(jax.random.normal(key_off, (NOCC, NOCC), jnp.float32), -4.0, 4.0) * 0.15
    symmetric = jnp.clip((raw + raw.T) * 0.7071, -0.5, 0.5)
    diag = -jax.random.uniform(key_diag, (NOCC,), jnp.float32, 0.5, 2.0)
    eye = jnp.eye(NOCC, dtype=jnp.float32)
    return (symmetric * (1.0 - eye) + eye * diag[None, :]).astype(jnp.bfloat16)


def steps_of(key, extent, cuts, smallest, largest):
    level, own = 1.0, jax.random.fold_in(key, 6)
    for position, blocks in cuts:
        steps = jnp.exp(jax.random.uniform(jax.random.fold_in(own, position), (blocks,), jnp.float32, smallest / len(cuts), largest / len(cuts)))
        level = level * jnp.repeat(steps, extent[position] // blocks).reshape([-1 if axis == position else 1 for axis in range(len(extent))])
    return level


def bell_draw(rng, dims, width, bound, cuts=(), held_as=jnp.bfloat16):
    factor_of = steps_of(rng, dims, cuts, -0.22, 0.18) if cuts else 1.0
    result = jax.random.normal(rng, dims, jnp.float32) * width * factor_of
    return jnp.minimum(jnp.maximum(result, -bound), bound).astype(held_as)


def setup_inputs(seed: int = 0) -> dict:
    seeds = jax.random.split(jax.random.key(seed), 10)
    integrals = bell_draw(seeds[0], (NAUX, NOCC, NV), (NAUX ** -0.25), 2.5, ((0, 8), (1, 4)))
    metric = bell_draw(seeds[1], (NAUX, NAUX), NAUX ** -0.5, 0.1875)
    fock = draw_fock(jax.random.fold_in(seeds[9], 71), 0)
    virt_energy = jnp.clip(jnp.exp(jax.random.uniform(seeds[3], (NV,), jnp.float32, math.log(0.3), math.log(3.0))), 0.3, 3.0)
    send_orb = draw_send_orb(jax.random.fold_in(seeds[9], 71), 0)
    pair_orb = draw_pair_orb(jax.random.fold_in(seeds[9], 71), 0)
    send_pair = draw_send_pair(jax.random.fold_in(seeds[9], 71), 0)
    cpl_slot = draw_cpl_slot(jax.random.fold_in(seeds[9], 71), 0)
    cpl_orb = draw_cpl_orb(jax.random.fold_in(seeds[9], 71), 0)
    return {"integrals": integrals, "metric": metric, "fock": fock, "virt_energy": virt_energy, "send_orb": send_orb, "pair_orb": pair_orb, "send_pair": send_pair, "cpl_slot": cpl_slot, "cpl_orb": cpl_orb}


def fitted_all(integrals, metric):
    flat = integrals.reshape(NAUX, NOCC * NV)
    fitted = jnp.dot(metric, flat, preferred_element_type=jnp.float32)
    return fitted.astype(jnp.bfloat16).reshape(NAUX, NOCC, NV)


def reference(integrals, metric, fock, virt_energy, send_orb, pair_orb, send_pair, cpl_slot, cpl_orb):
    fock = fock.astype(jnp.float32)
    ndev = N_AUX * N_GRP
    group_orbs = NOCC // N_GRP
    orb_dev = NOCC // ndev
    fitted = fitted_all(integrals, metric)
    device = (jnp.arange(ndev * PAIRS, dtype=jnp.int32) // PAIRS).astype(jnp.int32)
    column = device // N_GRP
    group = device % N_GRP

    def routed(orbital):
        source = orbital // group_orbs
        chosen = send_orb[column * N_GRP + source, group]
        return (source * group_orbs + column * orb_dev + chosen).astype(jnp.int32)

    orb_i = pair_orb[:, 0]
    orb_j = pair_orb[:, 1]
    src_i = routed(orb_i).reshape(ndev, PAIRS)
    src_j = routed(orb_j).reshape(ndev, PAIRS)

    def pair_block(args):
        left_idx, right_idx = args
        left = jnp.take(fitted, left_idx, axis=1).astype(jnp.float32)
        right = jnp.take(fitted, right_idx, axis=1).astype(jnp.float32)
        return jnp.einsum("qpa,qpb->pab", left, right)

    kmat = lax.map(pair_block, (src_i, src_j))
    diag_sum = (fock[orb_i, orb_i] + fock[orb_j, orb_j]).reshape(ndev, PAIRS)

    k_orb = cpl_orb[:, :, 0]
    l_orb = cpl_orb[:, :, 1]
    first = (l_orb == orb_j[:, None]) & (k_orb != orb_i[:, None])
    second = (k_orb == orb_i[:, None]) & (l_orb != orb_j[:, None])
    f_ik = fock[orb_i[:, None], k_orb]
    f_jl = fock[orb_j[:, None], l_orb]
    weight = (jnp.where(first, f_ik, jnp.float32(0.0)) + jnp.where(second, f_jl, jnp.float32(0.0))).reshape(ndev, PAIRS, NC)

    dev_ids = jnp.arange(ndev, dtype=jnp.int32)
    dev_col = dev_ids // N_GRP
    dev_grp = dev_ids % N_GRP
    sender = (dev_col[:, None] * N_GRP + jnp.arange(N_GRP, dtype=jnp.int32)[None, :]).astype(jnp.int32)
    qtab = (sender * PAIRS + send_pair[sender, dev_grp[:, None]]).astype(jnp.int32)
    slots = cpl_slot.reshape(ndev, PAIRS, NC)
    qpair = jnp.take_along_axis(jnp.broadcast_to(qtab[:, None, :], (ndev, PAIRS, N_GRP)), slots, axis=2)

    def denominator(dsum):
        return (virt_energy[:, None] + virt_energy[None, :])[None, :, :] - dsum[:, None, None]

    def start(args):
        kblk, dsum = args
        return -(kblk / denominator(dsum))

    amps = lax.map(start, (kmat, diag_sum))
    for step in range(ITERS):
        rounded = amps.astype(jnp.bfloat16).reshape(ndev * PAIRS, NV, NV)

        def update(args):
            kblk, ablk, dsum, wblk, qrow = args
            den = denominator(dsum)
            coupled = jnp.take(rounded, qrow.reshape(-1), axis=0).astype(jnp.float32).reshape(PAIRS, NC, NV, NV)
            term = jnp.einsum("pc,pcab->pab", wblk, coupled)
            resid = kblk + den * ablk - term
            return ablk - resid / den

        amps = lax.map(update, (kmat, amps, diag_sum, weight, qpair))
    return amps.reshape(ndev * PAIRS, NV, NV)
```

```python
import jax
import jax.numpy as jnp
from jax import lax
from jax.experimental import pallas as pl
from jax.experimental.pallas import tpu as pltpu
from jax.sharding import PartitionSpec as P

ITERS = 2


def final_kernel(idx_i, idx_j, mixing, diag, fit_ref, ve_col, ve_row, inc_ref, out_ref):
    p = pl.program_id(0)
    kmat = lax.dot_general(
        fit_ref[idx_i[p]],
        fit_ref[idx_j[p]],
        (((0,), (0,)), ((), ())),
        preferred_element_type=jnp.float32,
    )
    term = mixing[p, 0] * inc_ref[0].astype(jnp.float32)
    for s in range(1, inc_ref.shape[0]):
        term = term + mixing[p, s] * inc_ref[s].astype(jnp.float32)
    denom = (ve_col[...] + ve_row[...]) - diag[p]
    out_ref[0] = (term - kmat) / denom


def final_call(idx_i, idx_j, mixing, diag, fitted, virt_energy, incoming):
    pairs = idx_i.shape[0]
    nv = virt_energy.shape[0]
    whole = pl.BlockSpec(memory_space=pltpu.VMEM)
    return pl.pallas_call(
        final_kernel,
        out_shape=jax.ShapeDtypeStruct((pairs, nv, nv), jnp.float32),
        grid_spec=pltpu.PrefetchScalarGridSpec(
            num_scalar_prefetch=4,
            grid=(pairs,),
            in_specs=[whole, whole, whole, whole],
            out_specs=pl.BlockSpec((1, nv, nv), lambda p, *_: (p, 0, 0)),
        ),
    )(idx_i, idx_j, mixing, diag, fitted, virt_energy[:, None], virt_energy[None, :], incoming)


def on_device(
    integrals, metric, fock, virt_energy, send_orb, pair_orb, send_pair, cpl_slot, cpl_orb
):
    rows, group_orbs, nv = integrals.shape
    n_aux = lax.axis_size("aux")
    n_grp = lax.axis_size("grp")
    orb_dev = group_orbs // n_aux
    spread = jnp.broadcast_to(send_orb, (n_aux, n_grp))
    wanted = lax.all_to_all(spread, "aux", split_axis=0, concat_axis=0, tiled=True)
    idx = (jnp.arange(n_aux, dtype=jnp.int32)[:, None] * orb_dev + wanted).reshape(-1)
    packed = jnp.transpose(jnp.take(integrals, idx, axis=1, mode="clip"), (1, 0, 2))
    block = lax.all_to_all(packed, ("aux", "grp"), split_axis=0, concat_axis=0, tiled=True)
    block = block.reshape(n_aux, n_grp, rows, nv)
    block = jnp.transpose(block, (0, 2, 1, 3)).reshape(n_aux * rows, n_grp * nv)
    fitted = jnp.dot(metric, block, preferred_element_type=jnp.float32).astype(jnp.bfloat16)
    fitted = jnp.transpose(fitted.reshape(n_aux * rows, n_grp, nv), (1, 0, 2))

    orb_i = pair_orb[:, 0]
    orb_j = pair_orb[:, 1]
    idx_i = orb_i // group_orbs
    idx_j = orb_j // group_orbs
    diag_sum = fock[orb_i, orb_i].astype(jnp.float32) + fock[orb_j, orb_j].astype(jnp.float32)
    k_orb = cpl_orb[:, :, 0]
    l_orb = cpl_orb[:, :, 1]
    first = (l_orb == orb_j[:, None]) & (k_orb != orb_i[:, None])
    second = (k_orb == orb_i[:, None]) & (l_orb != orb_j[:, None])
    f_ik = fock[orb_i[:, None], k_orb].astype(jnp.float32)
    f_jl = fock[orb_j[:, None], l_orb].astype(jnp.float32)
    weight = jnp.where(first, f_ik, 0.0) + jnp.where(second, f_jl, 0.0)
    onehot = cpl_slot[:, :, None] == jnp.arange(n_grp, dtype=jnp.int32)[None, None, :]
    mixing = jnp.sum(jnp.where(onehot, weight[:, :, None], 0.0), axis=1)

    sent = send_pair[0]
    zeros = jnp.zeros((n_grp, nv, nv), jnp.bfloat16)
    s_i, s_j, s_mix, s_diag = idx_i[sent], idx_j[sent], mixing[sent], diag_sum[sent]
    incoming = zeros
    for step in range(ITERS):
        amps = final_call(s_i, s_j, s_mix, s_diag, fitted, virt_energy, incoming)
        incoming = lax.all_to_all(
            amps.astype(jnp.bfloat16), "grp", split_axis=0, concat_axis=0, tiled=True
        )
    return final_call(idx_i, idx_j, mixing, diag_sum, fitted, virt_energy, incoming)


def solution(mesh):
    in_specs = (
        P("aux", "grp", None),
        P(),
        P(),
        P(),
        P(("aux", "grp"), None),
        P(("aux", "grp"), None),
        P(("aux", "grp"), None),
        P(("aux", "grp"), None),
        P(("aux", "grp"), None, None),
    )
    out_specs = P(("aux", "grp"), None, None)
    return jax.shard_map(
        on_device, mesh=mesh, in_specs=in_specs, out_specs=out_specs, check_vma=False
    )
```

```python
import functools

import jax
import jax.numpy as jnp
from jax import lax
from jax.experimental import pallas as pl
from jax.experimental.pallas import tpu as pltpu
from jax.sharding import PartitionSpec as P

ITERS = 2
F32 = jnp.float32
BF16 = jnp.bfloat16
MESH = pl.DeviceIdType.MESH


def partner(me, step, size):
    out, bit = 0, 1
    while bit < size:
        out = out + (me // bit % 2 + step // bit % 2) % 2 * bit
        bit *= 2
    return out


def comm_kernel(
    n_aux, n_grp, orb_dev,
    pair_sm, send_sm, ints_hbm, metric_hbm, fock_ref, ve_ref, sorb_ref, pair_ref, slot_ref, corb_ref,
    kout, inc_out, mixb, dsumb, base,
    vint, vmet, svbuf, packed, recv, acc, fit_t, kbuf, ksent, sent_a, inc_a,
    sv_send, sv_recv, blk_send, blk_recv, amp_send, amp_recv, load_sem, kout_sem,
):
    me_a, me_g = lax.axis_index("aux"), lax.axis_index("grp")
    rows, group_orbs, nv = vint.shape
    naux = n_aux * rows
    pairs = pair_ref.shape[0]
    load_i = pltpu.make_async_copy(ints_hbm, vint, load_sem.at[0])
    load_m = pltpu.make_async_copy(metric_hbm, vmet, load_sem.at[1])
    load_i.start()
    load_m.start()
    for g in range(n_grp):
        svbuf[me_a, g * 8 : (g + 1) * 8, :] = jnp.broadcast_to(sorb_ref[0:1, g : g + 1], (8, 128))

    barrier = pltpu.get_barrier_semaphore()
    total = n_aux * n_grp

    def greet(t, carry):
        who = (partner(me_a, t // n_grp, n_aux), partner(me_g, t % n_grp, n_grp))
        pl.semaphore_signal(barrier, inc=1, device_id=who, device_id_type=MESH)
        return carry

    lax.fori_loop(1, total, greet, 0)
    pl.semaphore_wait(barrier, total - 1)

    def sv_copy(src, to):
        return pltpu.make_async_remote_copy(
            src_ref=svbuf.at[src], dst_ref=svbuf.at[src], send_sem=sv_send.at[to],
            recv_sem=sv_recv.at[src], device_id=(to, me_g), device_id_type=MESH,
        )

    for d in range(n_aux - 1, 0, -1):
        sv_copy(me_a, partner(me_a, d, n_aux)).start()

    orb_i, orb_j = pair_ref[:, 0:1], pair_ref[:, 1:2]
    nocc = fock_ref.shape[0]
    lane = lax.broadcasted_iota(jnp.int32, (pairs, nocc), 1)
    hot_i, hot_j = lane == orb_i, lane == orb_j
    row_i = jnp.dot(hot_i.astype(F32).astype(BF16), fock_ref[...], preferred_element_type=F32)
    row_j = jnp.dot(hot_j.astype(F32).astype(BF16), fock_ref[...], preferred_element_type=F32)
    pick = lambda hot, row: jnp.sum(jnp.where(hot, row, 0.0), axis=1, keepdims=True)
    dsum = pick(hot_i, row_i) + pick(hot_j, row_j)
    dsumb[...] = jnp.broadcast_to(dsum, (pairs, nv))
    mix = [jnp.zeros((pairs, 1), F32) for _ in range(n_grp)]
    for e in range(slot_ref.shape[1]):
        k_orb, l_orb = corb_ref[:, 2 * e : 2 * e + 1], corb_ref[:, 2 * e + 1 : 2 * e + 2]
        f_ik, f_jl = pick(lane == k_orb, row_i), pick(lane == l_orb, row_j)
        same_i, same_j = k_orb == orb_i, l_orb == orb_j
        weight = jnp.where(same_j, jnp.where(same_i, 0.0, f_ik), jnp.where(same_i, f_jl, 0.0))
        slot = slot_ref[:, e : e + 1]
        for s in range(n_grp):
            mix[s] = mix[s] + jnp.where(slot == s, weight, 0.0)
    for s in range(n_grp):
        mixb[s] = jnp.broadcast_to(mix[s], (pairs, nv))
    energy = jnp.broadcast_to(ve_ref[...], (nv, nv))
    base[...] = jnp.transpose(energy) + energy

    width = max(16, orb_dev)
    chunk = 256 // width
    depth = chunk * width
    sel_lane = lax.broadcasted_iota(jnp.int32, (chunk, depth), 1)
    same_row = lax.broadcasted_iota(jnp.int32, (chunk, depth), 0) == sel_lane // width
    sel_orb = sel_lane % width

    def pack(c):
        tile = pl.multiple_of(c * orb_dev // width * width, width)
        off = c * orb_dev - tile
        parts = []
        for g in range(n_grp):
            want = svbuf[c, g * 8 : (g + 1) * 8, :]
            want = jnp.concatenate([want] * (chunk // 8), axis=0)
            want = jnp.concatenate([want] * (depth // 128), axis=1)
            hit = same_row & (sel_orb == want + off)
            parts.append(jnp.where(hit, 1.0, 0.0).astype(BF16))
        sel = jnp.concatenate(parts, axis=0)
        for r in range(0, rows, chunk):
            data = vint[r : r + chunk, pl.ds(tile, width), :].reshape(depth, nv)
            got = jnp.dot(sel, data, preferred_element_type=F32).astype(BF16)
            packed[c, :, r : r + chunk, :] = got.reshape(n_grp, chunk, nv)

    def blk_copy(c, g):
        return pltpu.make_async_remote_copy(
            src_ref=packed.at[c, g], dst_ref=recv.at[me_g, pl.ds(pl.multiple_of(me_a * rows, rows), rows), :],
            send_sem=blk_send.at[c, g], recv_sem=blk_recv.at[me_a, me_g],
            device_id=(c, g), device_id_type=MESH,
        )

    def send_col(d):
        c = partner(me_a, d, n_aux)

        def one(k, carry):
            blk_copy(c, partner(me_g, n_grp - 1 - k, n_grp)).start()
            return carry

        lax.fori_loop(0, n_grp - 1, one, 0)

        @pl.when(d > 0)
        def _():
            blk_copy(c, me_g).start()

    def prepare(d):
        c = partner(me_a, d, n_aux)

        @pl.when(d > 0)
        def _():
            sv_copy(c, me_a).wait_recv()

        pack(c)

    load_i.wait()
    prepare(n_aux - 1)

    def feed(k, carry):
        d = n_aux - 1 - k
        prepare(d - 1)
        send_col(d)
        return carry

    lax.fori_loop(0, n_aux - 1, feed, 0)
    own = pltpu.make_async_copy(
        packed.at[me_a, me_g], recv.at[me_g, pl.ds(pl.multiple_of(me_a * rows, rows), rows), :], blk_recv.at[me_a, me_g]
    )
    send_col(0)
    own.start()
    load_m.wait()

    def await_blk(c, g):
        pltpu.make_async_remote_copy(
            src_ref=packed.at[c, g], dst_ref=recv.at[g, pl.ds(pl.multiple_of(c * rows, rows), rows), :],
            send_sem=blk_send.at[c, g], recv_sem=blk_recv.at[c, g],
            device_id=(c, g), device_id_type=MESH,
        ).wait_recv()

    half = n_aux // 2
    order = list(range(half - 1, 1, -1)) + [0, 1]
    span = 2 * rows
    tile_q = 256
    n_tiles = naux // tile_q
    for at, d2 in enumerate(order):
        chip = partner(me_a // 2, d2, half)
        start = pl.multiple_of(chip * span, span)

        def arrive(t, carry, d2=d2):
            c = partner(me_a, 2 * d2 + t // n_grp, n_aux)
            await_blk(c, partner(me_g, t % n_grp, n_grp))
            return carry

        if d2 == 0:
            own.wait()
        lax.fori_loop(1 if d2 == 0 else 0, 2 * n_grp, arrive, 0)

        def fit(s, carry, at=at, start=start):
            data = recv[s, pl.ds(start, span), :]
            for q in range(n_tiles):
                part = jnp.dot(
                    vmet[q * tile_q : (q + 1) * tile_q, pl.ds(start, span)], data, preferred_element_type=F32
                )
                if at:
                    part = part + acc[s, q * tile_q : (q + 1) * tile_q, :]
                if at < half - 1:
                    acc[s, q * tile_q : (q + 1) * tile_q, :] = part
                else:
                    recv[s, q * tile_q : (q + 1) * tile_q, :] = part.astype(BF16)
                    fit_t[s, :, q * tile_q : (q + 1) * tile_q] = jnp.transpose(part).astype(BF16)
            return carry

        lax.fori_loop(0, n_grp, fit, 0)

    def kmat(p):
        left = fit_t[pair_sm[p, 0] // group_orbs]
        right = recv[pair_sm[p, 1] // group_orbs]
        return jnp.dot(left, right, preferred_element_type=F32)

    def amp_copy(step, src_g, to_g):
        dst = inc_out if step == ITERS - 1 else inc_a.at[step]
        return pltpu.make_async_remote_copy(
            src_ref=sent_a.at[step, to_g], dst_ref=dst.at[src_g],
            send_sem=amp_send.at[step, to_g], recv_sem=amp_recv.at[step, src_g],
            device_id=(me_a, to_g), device_id_type=MESH,
        )

    def amp_own(step):
        dst = inc_out if step == ITERS - 1 else inc_a.at[step]
        return pltpu.make_async_copy(sent_a.at[step, me_g], dst.at[me_g], amp_recv.at[step, me_g])

    for step in range(ITERS):

        def amps(k, carry, step=step):
            g = partner(me_g, n_grp - 1 - k, n_grp)
            p = send_sm[0, g]
            if step == 0:
                val = kmat(p)
                ksent[g] = val
                top = -val
            else:
                top = -ksent[g]
                for s in range(n_grp):
                    top = top + mixb[s, pl.ds(p, 1), :] * inc_a[step - 1, s].astype(F32)
            sent_a[step, g] = (top / (base[...] - dsumb[pl.ds(p, 1), :])).astype(BF16)

            @pl.when(k > 0)
            def _():
                amp_copy(step, me_g, partner(me_g, n_grp - k, n_grp)).start()

            return carry

        lax.fori_loop(0, n_grp, amps, 0)
        amp_own(step).start()
        if step == 0:

            def all_k(p, carry):
                kbuf[p] = kmat(p)

                @pl.when(p > 0)
                def _():
                    pltpu.make_async_copy(kbuf.at[p - 1], kout.at[p - 1], kout_sem.at[p - 1]).start()

                return carry

            lax.fori_loop(0, pairs, all_k, 0)
            pltpu.make_async_copy(kbuf.at[pairs - 1], kout.at[pairs - 1], kout_sem.at[pairs - 1]).start()
        amp_own(step).wait()

        def arrived(k, carry, step=step):
            amp_copy(step, partner(me_g, k, n_grp), me_g).wait_recv()
            return carry

        lax.fori_loop(1, n_grp, arrived, 0)

    def kdone(p, carry):
        pltpu.make_async_copy(kbuf.at[p], kout.at[p], kout_sem.at[p]).wait()
        return carry

    lax.fori_loop(0, pairs, kdone, 0)
    for d in range(1, n_aux):
        sv_copy(me_a, partner(me_a, d, n_aux)).wait_send()

    def drain(t, carry):
        blk_copy(partner(me_a, t // n_grp, n_aux), partner(me_g, t % n_grp, n_grp)).wait_send()
        return carry

    lax.fori_loop(1, total, drain, 0)
    for step in range(ITERS):

        def sent(k, carry, step=step):
            amp_copy(step, me_g, partner(me_g, k, n_grp)).wait_send()
            return carry

        lax.fori_loop(1, n_grp, sent, 0)


def final_kernel(k_ref, mixb, dsumb, base, inc_ref, out_ref):
    p = pl.program_id(0)
    top = -k_ref[0]
    for s in range(inc_ref.shape[0]):
        top = top + mixb[s, pl.ds(p, 1), :] * inc_ref[s].astype(F32)
    out_ref[0] = top / (base[...] - dsumb[pl.ds(p, 1), :])


def on_device(
    integrals, metric, fock, virt_energy, send_orb, pair_orb, send_pair, cpl_slot, cpl_orb
):
    rows, group_orbs, nv = integrals.shape
    n_aux = lax.axis_size("aux")
    n_grp = lax.axis_size("grp")
    naux = metric.shape[0]
    pairs, n_cpl = cpl_slot.shape
    orb_dev = group_orbs // n_aux
    vmem = pl.BlockSpec(memory_space=pltpu.VMEM)
    smem = pl.BlockSpec(memory_space=pltpu.SMEM)
    anyspace = pl.BlockSpec(memory_space=pl.ANY)
    dma = pltpu.SemaphoreType.DMA
    kmats, incoming, mixb, dsumb, base = pl.pallas_call(
        functools.partial(comm_kernel, n_aux, n_grp, orb_dev),
        out_shape=(
            jax.ShapeDtypeStruct((pairs, nv, nv), F32),
            jax.ShapeDtypeStruct((n_grp, nv, nv), BF16),
            jax.ShapeDtypeStruct((n_grp, pairs, nv), F32),
            jax.ShapeDtypeStruct((pairs, nv), F32),
            jax.ShapeDtypeStruct((nv, nv), F32),
        ),
        in_specs=[smem, smem, anyspace, anyspace, vmem, vmem, vmem, vmem, vmem, vmem],
        out_specs=(anyspace, anyspace, vmem, vmem, vmem),
        scratch_shapes=[
            pltpu.VMEM((rows, group_orbs, nv), BF16),
            pltpu.VMEM((naux, naux), BF16),
            pltpu.VMEM((n_aux, n_grp * 8, 128), jnp.int32),
            pltpu.VMEM((n_aux, n_grp, rows, nv), BF16),
            pltpu.VMEM((n_grp, naux, nv), BF16),
            pltpu.VMEM((n_grp, naux, nv), F32),
            pltpu.VMEM((n_grp, nv, naux), BF16),
            pltpu.VMEM((pairs, nv, nv), F32),
            pltpu.VMEM((n_grp, nv, nv), F32),
            pltpu.VMEM((ITERS, n_grp, nv, nv), BF16),
            pltpu.VMEM((ITERS - 1, n_grp, nv, nv), BF16),
            dma((n_aux,)), dma((n_aux,)),
            dma((n_aux, n_grp)), dma((n_aux, n_grp)),
            dma((ITERS, n_grp)), dma((ITERS, n_grp)),
            dma((2,)), dma((pairs,)),
        ],
        compiler_params=pltpu.CompilerParams(
            collective_id=0, has_side_effects=True, vmem_limit_bytes=67043328
        ),
    )(
        pair_orb, send_pair, integrals, metric, fock, virt_energy[None, :], send_orb,
        pair_orb, cpl_slot, cpl_orb.reshape(pairs, 2 * n_cpl),
    )
    return pl.pallas_call(
        final_kernel,
        out_shape=jax.ShapeDtypeStruct((pairs, nv, nv), F32),
        grid=(pairs,),
        in_specs=[pl.BlockSpec((1, nv, nv), lambda p: (p, 0, 0)), vmem, vmem, vmem, vmem],
        out_specs=pl.BlockSpec((1, nv, nv), lambda p: (p, 0, 0)),
    )(kmats, mixb, dsumb, base, incoming)


def solution(mesh):
    in_specs = (
        P("aux", "grp", None),
        P(),
        P(),
        P(),
        P(("aux", "grp"), None),
        P(("aux", "grp"), None),
        P(("aux", "grp"), None),
        P(("aux", "grp"), None),
        P(("aux", "grp"), None, None),
    )
    out_specs = P(("aux", "grp"), None, None)
    return jax.shard_map(
        on_device, mesh=mesh, in_specs=in_specs, out_specs=out_specs, check_vma=False
    )
```

```python
import functools

import jax
import jax.numpy as jnp
from jax import lax
from jax.experimental import pallas as pl
from jax.experimental.pallas import tpu as pltpu
from jax.sharding import PartitionSpec as P

ITERS = 2
PARTS = 2
STRIP = 16
BLOCK = 32
F32 = jnp.float32
BF16 = jnp.bfloat16
MESH = pl.DeviceIdType.MESH


def partner(me, step, size):
    out, bit = 0, 1
    while bit < size:
        out = out + (me // bit % 2 + step // bit % 2) % 2 * bit
        bit *= 2
    return out


def comm_kernel(
    n_aux, n_grp, orb_dev,
    pair_sm, send_sm, ints_hbm, metric_hbm, fock_ref, ve_ref, sorb_ref, pair_ref, slot_ref, corb_ref,
    kout, inc_out, mixb, dsumb, base,
    vint, vmet, svbuf, packed, recv, acc, fit_t, kbuf, ksent, sent_a, inc_a,
    sv_send, sv_recv, blk_send, blk_recv, amp_send, amp_recv, load_sem, kout_sem,
):
    me_a, me_g = lax.axis_index("aux"), lax.axis_index("grp")
    rows, group_orbs, nv = vint.shape
    naux = n_aux * rows
    pairs = pair_ref.shape[1]
    load_i = pltpu.make_async_copy(ints_hbm, vint, load_sem.at[0])
    load_m = pltpu.make_async_copy(metric_hbm, vmet, load_sem.at[1])
    load_i.start()
    load_m.start()
    for g in range(n_grp):
        svbuf[me_a, g * 8 : (g + 1) * 8, :] = jnp.broadcast_to(sorb_ref[0:1, g : g + 1], (8, 128))

    barrier = pltpu.get_barrier_semaphore()
    total = n_aux * n_grp

    def greet(t, carry):
        who = (partner(me_a, t // n_grp, n_aux), partner(me_g, t % n_grp, n_grp))
        pl.semaphore_signal(barrier, inc=1, device_id=who, device_id_type=MESH)
        return carry

    lax.fori_loop(1, total, greet, 0)
    pl.semaphore_wait(barrier, total - 1)

    def sv_copy(src, to):
        return pltpu.make_async_remote_copy(
            src_ref=svbuf.at[src], dst_ref=svbuf.at[src], send_sem=sv_send.at[to],
            recv_sem=sv_recv.at[src], device_id=(to, me_g), device_id_type=MESH,
        )

    for d in range(n_aux - 1, 0, -1):
        sv_copy(me_a, partner(me_a, d, n_aux)).start()

    orb_i, orb_j = pair_ref[0:1, :], pair_ref[1:2, :]
    nocc = fock_ref.shape[0]
    orb = lax.broadcasted_iota(jnp.int32, (nocc, pairs), 0)
    eye = lax.broadcasted_iota(jnp.int32, (pairs, pairs), 0) == lax.broadcasted_iota(jnp.int32, (pairs, pairs), 1)
    ones = jnp.ones((pairs, nv), BF16)

    def fock_rows(hot):
        rhs = jnp.where(hot, 1.0, 0.0).astype(BF16)
        return lax.dot_general(fock_ref[...], rhs, (((0,), (0,)), ((), ())), preferred_element_type=F32)

    def spread(row):
        diagonal = jnp.where(eye, jnp.broadcast_to(row, (pairs, pairs)), 0.0).astype(BF16)
        return jnp.dot(diagonal, ones, preferred_element_type=F32)

    pick = lambda hot, row: jnp.sum(jnp.where(hot, row, 0.0), axis=0, keepdims=True)
    hot_i, hot_j = orb == orb_i, orb == orb_j
    row_i, row_j = fock_rows(hot_i), fock_rows(hot_j)
    dsumb[...] = spread(pick(hot_i, row_i)) + spread(pick(hot_j, row_j))
    mix = [jnp.zeros((1, pairs), F32) for _ in range(n_grp)]
    for e in range(slot_ref.shape[0]):
        k_orb, l_orb = corb_ref[2 * e : 2 * e + 1, :], corb_ref[2 * e + 1 : 2 * e + 2, :]
        f_ik, f_jl = pick(orb == k_orb, row_i), pick(orb == l_orb, row_j)
        same_i, same_j = k_orb == orb_i, l_orb == orb_j
        weight = jnp.where(same_j, jnp.where(same_i, 0.0, f_ik), jnp.where(same_i, f_jl, 0.0))
        slot = slot_ref[e : e + 1, :]
        for s in range(n_grp):
            mix[s] = mix[s] + jnp.where(slot == s, weight, 0.0)
    for s in range(n_grp):
        mixb[s] = spread(mix[s])
    energy = jnp.broadcast_to(ve_ref[...], (nv, nv))
    base[...] = jnp.transpose(energy) + energy

    width = max(16, orb_dev)
    chunk = 256 // width
    depth = chunk * width
    sel_lane = lax.broadcasted_iota(jnp.int32, (chunk, depth), 1)
    same_row = lax.broadcasted_iota(jnp.int32, (chunk, depth), 0) == sel_lane // width
    sel_orb = sel_lane % width

    def pack(c):
        tile = pl.multiple_of(c * orb_dev // width * width, width)
        off = c * orb_dev - tile
        parts = []
        for g in range(n_grp):
            want = svbuf[c, g * 8 : (g + 1) * 8, :]
            want = jnp.concatenate([want] * (chunk // 8), axis=0)
            want = jnp.concatenate([want] * (depth // 128), axis=1)
            hit = same_row & (sel_orb == want + off)
            parts.append(jnp.where(hit, 1.0, 0.0).astype(BF16))
        sel = jnp.concatenate(parts, axis=0)
        for r in range(0, rows, chunk):
            data = vint[r : r + chunk, pl.ds(tile, width), :].reshape(depth, nv)
            got = jnp.dot(sel, data, preferred_element_type=F32).astype(BF16)
            packed[c, :, r : r + chunk, :] = got.reshape(n_grp, chunk, nv)

    def blk_copy(c, g):
        return pltpu.make_async_remote_copy(
            src_ref=packed.at[c, g], dst_ref=recv.at[me_g, pl.ds(pl.multiple_of(me_a * rows, rows), rows), :],
            send_sem=blk_send.at[c, g], recv_sem=blk_recv.at[me_a, me_g],
            device_id=(c, g), device_id_type=MESH,
        )

    def send_col(d):
        c = partner(me_a, d, n_aux)

        def one(k, carry):
            blk_copy(c, partner(me_g, n_grp - 1 - k, n_grp)).start()
            return carry

        lax.fori_loop(0, n_grp - 1, one, 0)

        @pl.when(d > 0)
        def _():
            blk_copy(c, me_g).start()

    def prepare(d):
        c = partner(me_a, d, n_aux)

        @pl.when(d > 0)
        def _():
            sv_copy(c, me_a).wait_recv()

        pack(c)

    load_i.wait()
    prepare(n_aux - 1)

    def feed(k, carry):
        d = n_aux - 1 - k
        prepare(d - 1)
        send_col(d)
        return carry

    lax.fori_loop(0, n_aux - 1, feed, 0)
    own = pltpu.make_async_copy(
        packed.at[me_a, me_g], recv.at[me_g, pl.ds(pl.multiple_of(me_a * rows, rows), rows), :], blk_recv.at[me_a, me_g]
    )
    send_col(0)
    own.start()
    load_m.wait()

    def await_blk(c, g):
        pltpu.make_async_remote_copy(
            src_ref=packed.at[c, g], dst_ref=recv.at[g, pl.ds(pl.multiple_of(c * rows, rows), rows), :],
            send_sem=blk_send.at[c, g], recv_sem=blk_recv.at[c, g],
            device_id=(c, g), device_id_type=MESH,
        ).wait_recv()

    half = n_aux // 2
    order = list(range(half - 1, 1, -1)) + [0, 1]
    span = 2 * rows
    tile_q = 256
    n_tiles = naux // tile_q
    for at, d2 in enumerate(order):
        chip = partner(me_a // 2, d2, half)
        start = pl.multiple_of(chip * span, span)

        def arrive(t, carry, d2=d2):
            c = partner(me_a, 2 * d2 + t // n_grp, n_aux)
            await_blk(c, partner(me_g, t % n_grp, n_grp))
            return carry

        if d2 == 0:
            own.wait()
        lax.fori_loop(1 if d2 == 0 else 0, 2 * n_grp, arrive, 0)

        def fit(s, carry, at=at, start=start):
            data = recv[s, pl.ds(start, span), :]
            for q in range(n_tiles):
                part = jnp.dot(
                    vmet[q * tile_q : (q + 1) * tile_q, pl.ds(start, span)], data, preferred_element_type=F32
                )
                if at:
                    part = part + acc[s, q * tile_q : (q + 1) * tile_q, :]
                if at < half - 1:
                    acc[s, q * tile_q : (q + 1) * tile_q, :] = part
                else:
                    recv[s, q * tile_q : (q + 1) * tile_q, :] = part.astype(BF16)
                    fit_t[s, :, q * tile_q : (q + 1) * tile_q] = jnp.transpose(part).astype(BF16)
            return carry

        lax.fori_loop(0, n_grp, fit, 0)

    def kmat(p, r0=0, size=nv):
        left = fit_t[pair_sm[0, p] // group_orbs, r0 : r0 + size, :]
        right = recv[pair_sm[1, p] // group_orbs]
        return jnp.dot(left, right, preferred_element_type=F32)

    part_rows = nv // PARTS

    def amp_ref(step):
        return inc_out if step == ITERS - 1 else inc_a.at[step]

    def amp_copy(step, h, src_g, to_g):
        rows_h = pl.ds(h * part_rows, part_rows)
        return pltpu.make_async_remote_copy(
            src_ref=sent_a.at[step, to_g, rows_h, :], dst_ref=amp_ref(step).at[src_g, rows_h, :],
            send_sem=amp_send.at[step, h, to_g], recv_sem=amp_recv.at[step, h, src_g],
            device_id=(me_a, to_g), device_id_type=MESH,
        )

    def amp_own(step, h):
        rows_h = pl.ds(h * part_rows, part_rows)
        return pltpu.make_async_copy(
            sent_a.at[step, me_g, rows_h, :], amp_ref(step).at[me_g, rows_h, :], amp_recv.at[step, h, me_g]
        )

    def amp_wait(step, h):
        amp_own(step, h).wait()

        def arrived(k, carry):
            amp_copy(step, h, partner(me_g, k, n_grp), me_g).wait_recv()
            return carry

        lax.fori_loop(1, n_grp, arrived, 0)

    def k_blocks(lo, hi):
        def one(p, carry):
            kbuf[p] = kmat(p)

            @pl.when(p > lo)
            def _():
                pltpu.make_async_copy(kbuf.at[p - 1], kout.at[p - 1], kout_sem.at[p - 1]).start()

            return carry

        lax.fori_loop(lo, hi, one, 0)
        pltpu.make_async_copy(kbuf.at[hi - 1], kout.at[hi - 1], kout_sem.at[hi - 1]).start()

    for step in range(ITERS):
        for h in range(PARTS):
            if step:
                amp_wait(step - 1, h)

            def amps(k, carry, step=step, h=h):
                g = partner(me_g, n_grp - 1 - k, n_grp)
                p = send_sm[0, g]
                dsum_p = dsumb[pl.ds(p, 1), :]
                r0 = h * part_rows
                if step == 0:
                    ksent[g, r0 : r0 + part_rows, :] = kmat(p, r0, part_rows)
                mix_p = [mixb[s, pl.ds(p, 1), :] for s in range(n_grp)]
                for r in range(r0, r0 + part_rows, STRIP):
                    top = -ksent[g, r : r + STRIP, :]
                    if step:
                        for s in range(n_grp):
                            top = top + mix_p[s] * inc_a[step - 1, s, r : r + STRIP, :].astype(F32)
                    den = base[r : r + STRIP, :] - dsum_p
                    sent_a[step, g, r : r + STRIP, :] = (top / den).astype(BF16)

                @pl.when(k > 0)
                def _():
                    amp_copy(step, h, me_g, partner(me_g, n_grp - k, n_grp)).start()

                return carry

            lax.fori_loop(0, n_grp, amps, 0)
            amp_own(step, h).start()
        k_blocks(pairs * step // ITERS, pairs * (step + 1) // ITERS)
    for h in range(PARTS):
        amp_wait(ITERS - 1, h)

    def kdone(p, carry):
        pltpu.make_async_copy(kbuf.at[p], kout.at[p], kout_sem.at[p]).wait()
        return carry

    lax.fori_loop(0, pairs, kdone, 0)
    for d in range(1, n_aux):
        sv_copy(me_a, partner(me_a, d, n_aux)).wait_send()

    def drain(t, carry):
        blk_copy(partner(me_a, t // n_grp, n_aux), partner(me_g, t % n_grp, n_grp)).wait_send()
        return carry

    lax.fori_loop(1, total, drain, 0)
    for step in range(ITERS):
        for h in range(PARTS):

            def sent(k, carry, step=step, h=h):
                amp_copy(step, h, me_g, partner(me_g, k, n_grp)).wait_send()
                return carry

            lax.fori_loop(1, n_grp, sent, 0)


def final_kernel(k_ref, mixb, dsumb, base, inc_ref, out_ref):
    for r in range(0, k_ref.shape[1], STRIP):
        inc = [inc_ref[s, r : r + STRIP, :].astype(F32) for s in range(inc_ref.shape[0])]
        base_r = base[r : r + STRIP, :]
        for p in range(k_ref.shape[0]):
            top = -k_ref[p, r : r + STRIP, :]
            for s in range(len(inc)):
                top = top + mixb[s, p : p + 1, :] * inc[s]
            out_ref[p, r : r + STRIP, :] = top / (base_r - dsumb[p : p + 1, :])


def on_device(
    integrals, metric, fock, virt_energy, send_orb, pair_orb, send_pair, cpl_slot, cpl_orb
):
    rows, group_orbs, nv = integrals.shape
    n_aux = lax.axis_size("aux")
    n_grp = lax.axis_size("grp")
    naux = metric.shape[0]
    pairs, n_cpl = cpl_slot.shape
    orb_dev = group_orbs // n_aux
    pair_t = pair_orb.T
    cpl_t = jnp.transpose(cpl_orb, (1, 2, 0)).reshape(2 * n_cpl, pairs)
    vmem = pl.BlockSpec(memory_space=pltpu.VMEM)
    smem = pl.BlockSpec(memory_space=pltpu.SMEM)
    anyspace = pl.BlockSpec(memory_space=pl.ANY)
    dma = pltpu.SemaphoreType.DMA
    kmats, incoming, mixb, dsumb, base = pl.pallas_call(
        functools.partial(comm_kernel, n_aux, n_grp, orb_dev),
        out_shape=(
            jax.ShapeDtypeStruct((pairs, nv, nv), F32),
            jax.ShapeDtypeStruct((n_grp, nv, nv), BF16),
            jax.ShapeDtypeStruct((n_grp, pairs, nv), F32),
            jax.ShapeDtypeStruct((pairs, nv), F32),
            jax.ShapeDtypeStruct((nv, nv), F32),
        ),
        in_specs=[smem, smem, anyspace, anyspace, vmem, vmem, vmem, vmem, vmem, vmem],
        out_specs=(anyspace, anyspace, vmem, vmem, vmem),
        scratch_shapes=[
            pltpu.VMEM((rows, group_orbs, nv), BF16),
            pltpu.VMEM((naux, naux), BF16),
            pltpu.VMEM((n_aux, n_grp * 8, 128), jnp.int32),
            pltpu.VMEM((n_aux, n_grp, rows, nv), BF16),
            pltpu.VMEM((n_grp, naux, nv), BF16),
            pltpu.VMEM((n_grp, naux, nv), F32),
            pltpu.VMEM((n_grp, nv, naux), BF16),
            pltpu.VMEM((pairs, nv, nv), F32),
            pltpu.VMEM((n_grp, nv, nv), F32),
            pltpu.VMEM((ITERS, n_grp, nv, nv), BF16),
            pltpu.VMEM((ITERS - 1, n_grp, nv, nv), BF16),
            dma((n_aux,)), dma((n_aux,)),
            dma((n_aux, n_grp)), dma((n_aux, n_grp)),
            dma((ITERS, PARTS, n_grp)), dma((ITERS, PARTS, n_grp)),
            dma((2,)), dma((pairs,)),
        ],
        compiler_params=pltpu.CompilerParams(
            collective_id=0, has_side_effects=True, vmem_limit_bytes=67043328
        ),
    )(
        pair_t, send_pair, integrals, metric, fock, virt_energy[None, :], send_orb,
        pair_t, cpl_slot.T, cpl_t,
    )
    return pl.pallas_call(
        final_kernel,
        out_shape=jax.ShapeDtypeStruct((pairs, nv, nv), F32),
        grid=(nv // BLOCK,),
        in_specs=[
            pl.BlockSpec((pairs, BLOCK, nv), lambda i: (0, i, 0)),
            vmem,
            vmem,
            pl.BlockSpec((BLOCK, nv), lambda i: (i, 0)),
            pl.BlockSpec((n_grp, BLOCK, nv), lambda i: (0, i, 0)),
        ],
        out_specs=pl.BlockSpec((pairs, BLOCK, nv), lambda i: (0, i, 0)),
    )(kmats, mixb, dsumb, base, incoming)


def solution(mesh):
    in_specs = (
        P("aux", "grp", None),
        P(),
        P(),
        P(),
        P(("aux", "grp"), None),
        P(("aux", "grp"), None),
        P(("aux", "grp"), None),
        P(("aux", "grp"), None),
        P(("aux", "grp"), None, None),
    )
    out_specs = P(("aux", "grp"), None, None)
    return jax.shard_map(
        on_device, mesh=mesh, in_specs=in_specs, out_specs=out_specs, check_vma=False
    )
```

```python
import functools

import jax
import jax.numpy as jnp
from jax import lax
from jax.experimental import pallas as pl
from jax.experimental.pallas import tpu as pltpu
from jax.sharding import PartitionSpec as P

ITERS = 2
PARTS = 2
STRIP = 16
BLOCK = 128
F32 = jnp.float32
BF16 = jnp.bfloat16
MESH = pl.DeviceIdType.MESH


def partner(me, step, size):
    out, bit = 0, 1
    while bit < size:
        out = out + (me // bit % 2 + step // bit % 2) % 2 * bit
        bit *= 2
    return out


def comm_kernel(
    n_aux, n_grp, orb_dev,
    pair_sm, send_sm, ints_hbm, metric_hbm, fock_ref, ve_ref, sorb_ref, pair_ref, slot_ref, corb_ref,
    kout, inc_out, mixb, dsumb, base,
    vint, vmet, svbuf, packed, recv, acc, fit_t, kbuf, ksent, sent_a, inc_a,
    sv_send, sv_recv, blk_send, blk_recv, amp_send, amp_recv, load_sem, kout_sem,
):
    me_a, me_g = lax.axis_index("aux"), lax.axis_index("grp")
    rows, group_orbs, nv = vint.shape
    naux = n_aux * rows
    pairs = pair_ref.shape[1]
    load_i = pltpu.make_async_copy(ints_hbm, vint, load_sem.at[0])
    load_m = pltpu.make_async_copy(metric_hbm, vmet, load_sem.at[1])
    load_i.start()
    load_m.start()
    for g in range(n_grp):
        svbuf[me_a, g * 8 : (g + 1) * 8, :] = jnp.broadcast_to(sorb_ref[0:1, g : g + 1], (8, 128))

    barrier = pltpu.get_barrier_semaphore()
    total = n_aux * n_grp

    def greet(t, carry):
        who = (partner(me_a, t // n_grp, n_aux), partner(me_g, t % n_grp, n_grp))
        pl.semaphore_signal(barrier, inc=1, device_id=who, device_id_type=MESH)
        return carry

    lax.fori_loop(1, total, greet, 0)
    pl.semaphore_wait(barrier, total - 1)

    def sv_copy(src, to):
        return pltpu.make_async_remote_copy(
            src_ref=svbuf.at[src], dst_ref=svbuf.at[src], send_sem=sv_send.at[to],
            recv_sem=sv_recv.at[src], device_id=(to, me_g), device_id_type=MESH,
        )

    for d in range(n_aux - 1, 0, -1):
        sv_copy(me_a, partner(me_a, d, n_aux)).start()

    orb_i, orb_j = pair_ref[0:1, :], pair_ref[1:2, :]
    nocc = fock_ref.shape[0]
    orb = lax.broadcasted_iota(jnp.int32, (nocc, pairs), 0)
    eye = lax.broadcasted_iota(jnp.int32, (pairs, pairs), 0) == lax.broadcasted_iota(jnp.int32, (pairs, pairs), 1)
    ones = jnp.ones((pairs, nv), BF16)

    def fock_rows(hot):
        rhs = jnp.where(hot, 1.0, 0.0).astype(BF16)
        return lax.dot_general(fock_ref[...], rhs, (((0,), (0,)), ((), ())), preferred_element_type=F32)

    def spread(row):
        diagonal = jnp.where(eye, jnp.broadcast_to(row, (pairs, pairs)), 0.0).astype(BF16)
        return jnp.dot(diagonal, ones, preferred_element_type=F32)

    pick = lambda hot, row: jnp.sum(jnp.where(hot, row, 0.0), axis=0, keepdims=True)
    hot_i, hot_j = orb == orb_i, orb == orb_j
    row_i, row_j = fock_rows(hot_i), fock_rows(hot_j)
    dsumb[...] = spread(pick(hot_i, row_i)) + spread(pick(hot_j, row_j))
    mix = [jnp.zeros((1, pairs), F32) for _ in range(n_grp)]
    for e in range(slot_ref.shape[0]):
        k_orb, l_orb = corb_ref[2 * e : 2 * e + 1, :], corb_ref[2 * e + 1 : 2 * e + 2, :]
        f_ik, f_jl = pick(orb == k_orb, row_i), pick(orb == l_orb, row_j)
        same_i, same_j = k_orb == orb_i, l_orb == orb_j
        weight = jnp.where(same_j, jnp.where(same_i, 0.0, f_ik), jnp.where(same_i, f_jl, 0.0))
        slot = slot_ref[e : e + 1, :]
        for s in range(n_grp):
            mix[s] = mix[s] + jnp.where(slot == s, weight, 0.0)
    for s in range(n_grp):
        mixb[s] = spread(mix[s])
    energy = jnp.broadcast_to(ve_ref[...], (nv, nv))
    base[...] = jnp.transpose(energy) + energy

    width = max(16, orb_dev)
    chunk = 256 // width
    depth = chunk * width
    sel_lane = lax.broadcasted_iota(jnp.int32, (chunk, depth), 1)
    same_row = lax.broadcasted_iota(jnp.int32, (chunk, depth), 0) == sel_lane // width
    sel_orb = sel_lane % width

    def pack(c):
        tile = pl.multiple_of(c * orb_dev // width * width, width)
        off = c * orb_dev - tile
        parts = []
        for g in range(n_grp):
            want = svbuf[c, g * 8 : (g + 1) * 8, :]
            want = jnp.concatenate([want] * (chunk // 8), axis=0)
            want = jnp.concatenate([want] * (depth // 128), axis=1)
            hit = same_row & (sel_orb == want + off)
            parts.append(jnp.where(hit, 1.0, 0.0).astype(BF16))
        sel = jnp.concatenate(parts, axis=0)
        for r in range(0, rows, chunk):
            data = vint[r : r + chunk, pl.ds(tile, width), :].reshape(depth, nv)
            got = jnp.dot(sel, data, preferred_element_type=F32).astype(BF16)
            packed[c, :, r : r + chunk, :] = got.reshape(n_grp, chunk, nv)

    def blk_copy(c, g):
        return pltpu.make_async_remote_copy(
            src_ref=packed.at[c, g], dst_ref=recv.at[me_g, pl.ds(pl.multiple_of(me_a * rows, rows), rows), :],
            send_sem=blk_send.at[c, g], recv_sem=blk_recv.at[me_a, me_g],
            device_id=(c, g), device_id_type=MESH,
        )

    def send_col(d):
        c = partner(me_a, d, n_aux)

        def one(k, carry):
            blk_copy(c, partner(me_g, n_grp - 1 - k, n_grp)).start()
            return carry

        lax.fori_loop(0, n_grp - (d == 0), one, 0)

    def prepare(d):
        c = partner(me_a, d, n_aux)
        if d:
            sv_copy(c, me_a).wait_recv()
        pack(c)

    own = pltpu.make_async_copy(
        packed.at[me_a, me_g], recv.at[me_g, pl.ds(pl.multiple_of(me_a * rows, rows), rows), :], blk_recv.at[me_a, me_g]
    )
    half = n_aux // 2
    steps = [2 * d2 + core for d2 in [*range(1, half), 0] for core in (1, 0)]
    load_i.wait()
    prepare(steps[0])
    for d, after in zip(steps, steps[1:] + [None]):
        if after is not None:
            prepare(after)
        send_col(d)
    own.start()
    load_m.wait()

    def await_blk(c, g):
        pltpu.make_async_remote_copy(
            src_ref=packed.at[c, g], dst_ref=recv.at[g, pl.ds(pl.multiple_of(c * rows, rows), rows), :],
            send_sem=blk_send.at[c, g], recv_sem=blk_recv.at[c, g],
            device_id=(c, g), device_id_type=MESH,
        ).wait_recv()

    order = [1, 0, *range(2, half)]
    span = 2 * rows
    tile_q = 256
    n_tiles = naux // tile_q
    for at, d2 in enumerate(order):
        chip = partner(me_a // 2, d2, half)
        start = pl.multiple_of(chip * span, span)

        def arrive(t, carry, d2=d2):
            c = partner(me_a, 2 * d2 + t // n_grp, n_aux)
            await_blk(c, partner(me_g, t % n_grp, n_grp))
            return carry

        if d2 == 0:
            own.wait()
        lax.fori_loop(1 if d2 == 0 else 0, 2 * n_grp, arrive, 0)

        def fit(s, carry, at=at, start=start):
            data = recv[s, pl.ds(start, span), :]
            for q in range(n_tiles):
                part = jnp.dot(
                    vmet[q * tile_q : (q + 1) * tile_q, pl.ds(start, span)], data, preferred_element_type=F32
                )
                if at:
                    part = part + acc[s, q * tile_q : (q + 1) * tile_q, :]
                if at < half - 1:
                    acc[s, q * tile_q : (q + 1) * tile_q, :] = part
                else:
                    recv[s, q * tile_q : (q + 1) * tile_q, :] = part.astype(BF16)
                    fit_t[s, :, q * tile_q : (q + 1) * tile_q] = jnp.transpose(part).astype(BF16)
            return carry

        lax.fori_loop(0, n_grp, fit, 0)

    def kmat(p, r0=0, size=nv):
        left = fit_t[pair_sm[0, p] // group_orbs, r0 : r0 + size, :]
        right = recv[pair_sm[1, p] // group_orbs]
        return jnp.dot(left, right, preferred_element_type=F32)

    part_rows = nv // PARTS

    def amp_ref(step):
        return inc_out if step == ITERS - 1 else inc_a.at[step]

    def amp_copy(step, h, src_g, to_g):
        rows_h = pl.ds(h * part_rows, part_rows)
        return pltpu.make_async_remote_copy(
            src_ref=sent_a.at[step, to_g, rows_h, :], dst_ref=amp_ref(step).at[src_g, rows_h, :],
            send_sem=amp_send.at[step, h, to_g], recv_sem=amp_recv.at[step, h, src_g],
            device_id=(me_a, to_g), device_id_type=MESH,
        )

    def amp_own(step, h):
        rows_h = pl.ds(h * part_rows, part_rows)
        return pltpu.make_async_copy(
            sent_a.at[step, me_g, rows_h, :], amp_ref(step).at[me_g, rows_h, :], amp_recv.at[step, h, me_g]
        )

    def amp_wait(step, h):
        amp_own(step, h).wait()

        def arrived(k, carry):
            amp_copy(step, h, partner(me_g, k, n_grp), me_g).wait_recv()
            return carry

        lax.fori_loop(1, n_grp, arrived, 0)

    def k_blocks(lo, hi):
        def one(p, carry):
            kbuf[p] = kmat(p)

            @pl.when(p > lo)
            def _():
                pltpu.make_async_copy(kbuf.at[p - 1], kout.at[p - 1], kout_sem.at[p - 1]).start()

            return carry

        lax.fori_loop(lo, hi, one, 0)
        pltpu.make_async_copy(kbuf.at[hi - 1], kout.at[hi - 1], kout_sem.at[hi - 1]).start()

    for step in range(ITERS):
        for h in range(PARTS):
            if step:
                amp_wait(step - 1, h)

            def amps(k, carry, step=step, h=h):
                g = partner(me_g, n_grp - 1 - k, n_grp)
                p = send_sm[0, g]
                dsum_p = dsumb[pl.ds(p, 1), :]
                r0 = h * part_rows
                if step == 0:
                    ksent[g, r0 : r0 + part_rows, :] = kmat(p, r0, part_rows)
                mix_p = [mixb[s, pl.ds(p, 1), :] for s in range(n_grp)]
                for r in range(r0, r0 + part_rows, STRIP):
                    top = -ksent[g, r : r + STRIP, :]
                    if step:
                        for s in range(n_grp):
                            top = top + mix_p[s] * inc_a[step - 1, s, r : r + STRIP, :].astype(F32)
                    den = base[r : r + STRIP, :] - dsum_p
                    sent_a[step, g, r : r + STRIP, :] = (top / den).astype(BF16)

                @pl.when(k > 0)
                def _():
                    amp_copy(step, h, me_g, partner(me_g, n_grp - k, n_grp)).start()

                return carry

            lax.fori_loop(0, n_grp, amps, 0)
            amp_own(step, h).start()
        k_blocks(pairs * step // ITERS, pairs * (step + 1) // ITERS)
    for h in range(PARTS):
        amp_wait(ITERS - 1, h)

    def kdone(p, carry):
        pltpu.make_async_copy(kbuf.at[p], kout.at[p], kout_sem.at[p]).wait()
        return carry

    lax.fori_loop(0, pairs, kdone, 0)
    for d in range(1, n_aux):
        sv_copy(me_a, partner(me_a, d, n_aux)).wait_send()

    def drain(t, carry):
        blk_copy(partner(me_a, t // n_grp, n_aux), partner(me_g, t % n_grp, n_grp)).wait_send()
        return carry

    lax.fori_loop(1, total, drain, 0)
    for step in range(ITERS):
        for h in range(PARTS):

            def sent(k, carry, step=step, h=h):
                amp_copy(step, h, me_g, partner(me_g, k, n_grp)).wait_send()
                return carry

            lax.fori_loop(1, n_grp, sent, 0)


def final_kernel(k_ref, mixb, dsumb, base, inc_ref, out_ref):
    for r in range(0, k_ref.shape[1], STRIP):
        inc = [inc_ref[s, r : r + STRIP, :].astype(F32) for s in range(inc_ref.shape[0])]
        base_r = base[r : r + STRIP, :]
        for p in range(k_ref.shape[0]):
            top = -k_ref[p, r : r + STRIP, :]
            for s in range(len(inc)):
                top = top + mixb[s, p : p + 1, :] * inc[s]
            out_ref[p, r : r + STRIP, :] = top / (base_r - dsumb[p : p + 1, :])


def on_device(
    integrals, metric, fock, virt_energy, send_orb, pair_orb, send_pair, cpl_slot, cpl_orb
):
    rows, group_orbs, nv = integrals.shape
    n_aux = lax.axis_size("aux")
    n_grp = lax.axis_size("grp")
    naux = metric.shape[0]
    pairs, n_cpl = cpl_slot.shape
    orb_dev = group_orbs // n_aux
    pair_t = pair_orb.T
    cpl_t = jnp.transpose(cpl_orb, (1, 2, 0)).reshape(2 * n_cpl, pairs)
    vmem = pl.BlockSpec(memory_space=pltpu.VMEM)
    smem = pl.BlockSpec(memory_space=pltpu.SMEM)
    anyspace = pl.BlockSpec(memory_space=pl.ANY)
    dma = pltpu.SemaphoreType.DMA
    kmats, incoming, mixb, dsumb, base = pl.pallas_call(
        functools.partial(comm_kernel, n_aux, n_grp, orb_dev),
        out_shape=(
            jax.ShapeDtypeStruct((pairs, nv, nv), F32),
            jax.ShapeDtypeStruct((n_grp, nv, nv), BF16),
            jax.ShapeDtypeStruct((n_grp, pairs, nv), F32),
            jax.ShapeDtypeStruct((pairs, nv), F32),
            jax.ShapeDtypeStruct((nv, nv), F32),
        ),
        in_specs=[smem, smem, anyspace, anyspace, vmem, vmem, vmem, vmem, vmem, vmem],
        out_specs=(anyspace, anyspace, vmem, vmem, vmem),
        scratch_shapes=[
            pltpu.VMEM((rows, group_orbs, nv), BF16),
            pltpu.VMEM((naux, naux), BF16),
            pltpu.VMEM((n_aux, n_grp * 8, 128), jnp.int32),
            pltpu.VMEM((n_aux, n_grp, rows, nv), BF16),
            pltpu.VMEM((n_grp, naux, nv), BF16),
            pltpu.VMEM((n_grp, naux, nv), F32),
            pltpu.VMEM((n_grp, nv, naux), BF16),
            pltpu.VMEM((pairs, nv, nv), F32),
            pltpu.VMEM((n_grp, nv, nv), F32),
            pltpu.VMEM((ITERS, n_grp, nv, nv), BF16),
            pltpu.VMEM((ITERS - 1, n_grp, nv, nv), BF16),
            dma((n_aux,)), dma((n_aux,)),
            dma((n_aux, n_grp)), dma((n_aux, n_grp)),
            dma((ITERS, PARTS, n_grp)), dma((ITERS, PARTS, n_grp)),
            dma((2,)), dma((pairs,)),
        ],
        compiler_params=pltpu.CompilerParams(
            collective_id=0, has_side_effects=True, vmem_limit_bytes=67043328
        ),
    )(
        pair_t, send_pair, integrals, metric, fock, virt_energy[None, :], send_orb,
        pair_t, cpl_slot.T, cpl_t,
    )
    return pl.pallas_call(
        final_kernel,
        out_shape=jax.ShapeDtypeStruct((pairs, nv, nv), F32),
        grid=(nv // BLOCK,),
        in_specs=[
            pl.BlockSpec((pairs, BLOCK, nv), lambda i: (0, i, 0)),
            vmem,
            vmem,
            pl.BlockSpec((BLOCK, nv), lambda i: (i, 0)),
            pl.BlockSpec((n_grp, BLOCK, nv), lambda i: (0, i, 0)),
        ],
        out_specs=pl.BlockSpec((pairs, BLOCK, nv), lambda i: (0, i, 0)),
    )(kmats, mixb, dsumb, base, incoming)


def solution(mesh):
    in_specs = (
        P("aux", "grp", None),
        P(),
        P(),
        P(),
        P(("aux", "grp"), None),
        P(("aux", "grp"), None),
        P(("aux", "grp"), None),
        P(("aux", "grp"), None),
        P(("aux", "grp"), None, None),
    )
    out_specs = P(("aux", "grp"), None, None)
    return jax.shard_map(
        on_device, mesh=mesh, in_specs=in_specs, out_specs=out_specs, check_vma=False
    )
```
